256 devices in a mesh: lat: 4 (over z_lo, core), lon: 16 (over z_hi, y), tm: 4 (over x).
Axes of the slice: x: 4, y: 4, z: 8 (z_hi: 4, z_lo: 2; z = z_hi * 2 + z_lo), core: 2. Of those that a mesh axis runs over, the one named last changes fastest.
Arguments:
- signal: bfloat16 [4, 78, 32, 2048], P('tm', None, 'lat', 'lon'), may hold values from -6 to 6
- dictionary: bfloat16 [64, 9984], P('lon'), may hold values from -0.0625 to 0.0625
- codes_init: float32 [4, 64, 8, 512], P('tm', None, 'lat', 'lon'), may hold values from -3 to 3
- thresholds: float32 [64], replicated, may hold values from 0.2 to 2
Outputs:
- codes: float32 [4, 64, 8, 512], P('tm', None, 'lat', 'lon')
- dict_grad: float32 [64, 9984], P('lon')
The draws below stay inside these ranges and needn't reach their ends.
All inputs are finite; a program needn't handle non-finite values.
Results may differ from the reference program's by a relative error of at most 0.0044.
Values may be sent and summed in bfloat16 or wider, within the bound.
No kernel may reach another device: no remote copies, remote signals or barrier semaphores. Data moves between devices by JAX's collectives and lax.ppermute only.
A program may use at most 128 MiB of HBM per device.

```python
import math
import jax
import jax.numpy as jnp
from jax import lax

CHANNELS = 78
ATOMS = 64
ITERS = 2
ATOM_LEN = 9984
FRAMES = 4
HEIGHT = 32
WIDTH = 2048
PZ = 8
QZ = 512


def shard_levels(key, extent, shards, least, high):
    level, own = 1.0, jax.random.fold_in(key, 6)
    for dim, shards_of in shards:
        heights = jnp.exp(jax.random.uniform(jax.random.fold_in(own, dim), (shards_of,), jnp.float32, least / len(shards), high / len(shards)))
        level = level * jnp.repeat(heights, extent[dim] // shards_of).reshape([-1 if axis == dim else 1 for axis in range(len(extent))])
    return level


def scatter_about(rng, extent, scale, limit, split=(), held_as=jnp.bfloat16):
    factor_of = shard_levels(rng, extent, split, -0.22, 0.18) if split else 1.0
    entries = jax.random.normal(rng, extent, jnp.float32) * scale * factor_of
    return jnp.minimum(jnp.maximum(entries, -limit), limit).astype(held_as)


def setup_inputs(seed: int = 0) -> dict:
    streams_of = jax.random.split(jax.random.key(seed), 5)
    return {
        "signal": scatter_about(streams_of[0], (FRAMES, CHANNELS, HEIGHT, WIDTH), 1.0, 6.0, ((0, 4), (2, 4), (3, 16))),
        "dictionary": scatter_about(streams_of[1], (ATOMS, ATOM_LEN), ATOM_LEN ** -0.5, 0.0625, ((0, 16),)),
        "codes_init": scatter_about(streams_of[2], (FRAMES, ATOMS, PZ, QZ), 0.5, 3.0, ((0, 4), (2, 4), (3, 16)), jnp.float32),
        "thresholds": jnp.clip(jnp.exp(jax.random.uniform(streams_of[3], (ATOMS,), jnp.float32, math.log(0.2), math.log(2.0))), 0.2, 2.0),
    }


STEP_SIZE = 0.5

def shift_codes(codes, delay, down, right):
    moved = jnp.roll(codes, right, axis=3)
    if down:
        moved = jnp.concatenate([jnp.zeros_like(moved[:, :, :1]), moved[:, :, :-1]], axis=2)
    if delay:
        moved = jnp.concatenate([jnp.zeros_like(moved[:, :1]), moved[:, :-1]], axis=1)
    return moved

def shift_back(resid, delay, down, right):
    moved = jnp.roll(resid, -right, axis=3)
    if down:
        moved = jnp.concatenate([moved[:, :, 1:], jnp.zeros_like(moved[:, :, :1])], axis=2)
    if delay:
        moved = jnp.concatenate([moved[:, 1:], jnp.zeros_like(moved[:, :1])], axis=1)
    return moved

def reference(signal, dictionary, codes_init, thresholds):
    frames, channels, height, width = signal.shape
    rows = height // 4
    columns = width // 4
    patch = channels * 16
    atoms = dictionary.shape[0]
    blocks = dictionary.reshape(atoms, 2, channels, 2, 4, 2, 4).transpose(1, 3, 5, 2, 4, 6, 0).reshape(8, patch, atoms)
    target = signal.reshape(frames, channels, rows, 4, columns, 4).transpose(1, 3, 5, 0, 2, 4)
    target = target.reshape(patch, frames, rows, columns)
    combos = [(delay, down, right) for delay in (0, 1) for down in (0, 1) for right in (0, 1)]

    def residual_of(current):
        coded = current.astype(jnp.bfloat16)
        total = jnp.zeros((patch, frames * rows * columns), jnp.float32)
        for index, (delay, down, right) in enumerate(combos):
            moved = shift_codes(coded, delay, down, right).reshape(atoms, -1)
            total = total + jnp.dot(blocks[index], moved, preferred_element_type=jnp.float32)
        return ((total.reshape(target.shape) - target).astype(jnp.bfloat16), coded)

    def adjoint(resid):
        total = jnp.zeros((atoms, frames * rows * columns), jnp.float32)
        for index, (delay, down, right) in enumerate(combos):
            moved = shift_back(resid, delay, down, right).reshape(patch, -1)
            total = total + lax.dot_general(blocks[index], moved, (((0,), (0,)), ((), ())), preferred_element_type=jnp.float32)
        return total.reshape(atoms, frames, rows, columns)
    current = jnp.transpose(codes_init, (1, 0, 2, 3))
    moving = current
    momentum_now = 1.0
    shrink = STEP_SIZE * thresholds[:, None, None, None]
    for turn in range(ITERS):
        resid, coded = residual_of(moving)
        descent = moving - STEP_SIZE * adjoint(resid)
        updated = jnp.sign(descent) * jnp.maximum(jnp.abs(descent) - shrink, 0.0)
        momentum_next = (1.0 + math.sqrt(1.0 + 4.0 * momentum_now * momentum_now)) / 2.0
        moving = updated + (momentum_now - 1.0) / momentum_next * (updated - current)
        current = updated
        momentum_now = momentum_next
    resid, coded = residual_of(current)
    flat_resid = resid.reshape(patch, -1)
    pieces = []
    for index, (delay, down, right) in enumerate(combos):
        moved = shift_codes(coded, delay, down, right).reshape(atoms, -1)
        pieces.append(lax.dot_general(flat_resid, moved, (((1,), (1,)), ((), ())), preferred_element_type=jnp.float32))
    grads = jnp.stack(pieces).reshape(2, 2, 2, channels, 4, 4, atoms).transpose(6, 0, 3, 1, 4, 2, 5)
    scale = 1.0 / math.sqrt(frames * rows * columns)
    dict_grad = grads.reshape(atoms, 2 * channels * 64) * scale
    return (jnp.transpose(current, (1, 0, 2, 3)), dict_grad)
```

```python
import math

import jax
import jax.numpy as jnp
from jax import lax
from jax.experimental import pallas as pl
from jax.experimental.pallas import tpu as pltpu
from jax.sharding import PartitionSpec as P

ITERS = 2
STEP_SIZE = 0.5
F32 = jnp.float32
BF16 = jnp.bfloat16
GROUP = ("lat", "tm")
COMBOS = [(h, a, b) for h in (0, 1) for a in (0, 1) for b in (0, 1)]
MAIN = 1024
LANES = 1280
HALF = 320
PACK = 416


def iota(shape, dim):
    return lax.broadcasted_iota(jnp.int32, shape, dim)


def dot(a, b):
    return jnp.dot(a, b, preferred_element_type=F32)


def dot_t(a, b):
    return lax.dot_general(a, b, (((1,), (1,)), ((), ())), preferred_element_type=F32)


def onehot(test):
    return jnp.where(test, 1.0, 0.0).astype(BF16)


def three(x):
    high = x.astype(BF16)
    rest = x - high.astype(F32)
    middle = rest.astype(BF16)
    low = (rest - middle.astype(F32)).astype(BF16)
    return high, middle, low


def call(kernel, outs, name, scratch=(), smem=0, n_in=1):
    vmem = pl.BlockSpec(memory_space=pltpu.VMEM)
    specs = [pl.BlockSpec(memory_space=pltpu.SMEM)] * smem + [vmem] * (n_in - smem)
    shapes = [jax.ShapeDtypeStruct(s, d) for s, d in outs]
    return pl.pallas_call(
        kernel,
        out_shape=shapes if len(shapes) > 1 else shapes[0],
        in_specs=specs,
        out_specs=[vmem] * len(shapes) if len(shapes) > 1 else vmem,
        scratch_shapes=list(scratch),
        name=name,
        compiler_params=pltpu.CompilerParams(vmem_limit_bytes=48 * 1024 * 1024),
    )


def pack_kernel(x_ref, z_ref, out_ref):
    row, col = iota((128, 128), 0), iota((128, 128), 1)
    order = onehot(((row & 3) * 32 + (row >> 2)) == col)
    split = [dot(x_ref[r], order) for r in range(8)]
    lane = iota((80, 128), 1)
    high, middle, low = three(z_ref[...])
    first = jnp.concatenate([high.astype(F32), middle[:32].astype(F32)], axis=0)
    second = jnp.concatenate([middle[32:].astype(F32), low.astype(F32)], axis=0)
    codes = jnp.concatenate([first, second], axis=1).astype(BF16)
    for core in range(2):
        for v in range(4):
            piece = jnp.zeros((80, 128), F32)
            for u_lo in range(2):
                for p2 in range(2):
                    slot = u_lo * 2 + p2
                    source = split[p2 * 4 + core * 2 + u_lo]
                    by = ((slot - v) % 4) * 32
                    moved = pltpu.roll(source, by, 1) if by else source
                    piece = jnp.where((lane >> 5) == slot, moved, piece)
            piece = piece.astype(BF16)
            for z in range(2):
                for t in range(4):
                    out_ref[(2 * z + core) * 4 + t, v * 80 : v * 80 + 80, :] = piece
        for z in range(2):
            for t in range(4):
                out_ref[(2 * z + core) * 4 + t, HALF:PACK, :] = codes


def unpack_kernel(in_ref, main_ref, first_ref, last_ref, left_ref):
    lane = iota((PACK, 128), 1)
    for pair in range(8):
        even = in_ref[2 * pair].astype(F32)
        odd = in_ref[2 * pair + 1].astype(F32)
        lanes = slice(pair * 128, pair * 128 + 128)
        left_ref[0:PACK, lanes] = jnp.where(lane < 64, even, pltpu.roll(odd, 64, 1)).astype(BF16)
        left_ref[PACK : 2 * PACK, lanes] = jnp.where(lane < 64, pltpu.roll(even, 64, 1), odd).astype(BF16)
    for block in range(4):
        n = iota((1024, 256), 1) + block * 256
        source = (((n >> 1) & 3) * 4 + ((n >> 3) & 3)) * 64 + (n & 1) * 32 + (n >> 5)
        order = onehot(iota((1024, 256), 0) == source)
        main_ref[:, block * 256 : block * 256 + 256] = dot(left_ref[...], order).astype(BF16)
    first_ref[...] = main_ref[:, 0:128]
    last_ref[...] = main_ref[:, MAIN - 128 : MAIN]


def slice_kernel(place_ref, d_ref, out_ref, rows_ref):
    rows_ref[...] = jnp.zeros((512, 128), F32)
    for i in range(78):
        h, half = i // 39, i % 39
        part = d_ref[:, i * 128 : i * 128 + 128].astype(F32)
        for k in range(4):
            at = (k * 2 + h) * 64 + half
            rows_ref[at : at + 1, :] = part[k : k + 1, :]
    u, v = place_ref[0], place_ref[1]
    which = iota((8, 128), 0)
    want = (which >> 2) * 64 + ((which >> 1) & 1) * 32 + u * 8 + (which & 1) * 4 + v
    picked = dot_t(onehot(iota((8, 128), 1) == want), rows_ref[...].astype(BF16))
    lane = iota((4, 128), 1)
    result = [None] * 8
    for k in range(4):
        pair = picked[:, k * 128 : k * 128 + 128]
        turned = pltpu.roll(pair, 64, 1)
        result[k] = jnp.where(lane < 64, pair[0:4], turned[4:8])
        result[4 + k] = jnp.where(lane < 64, turned[0:4], pair[4:8])
    for h in range(2):
        for ab in range(4):
            for k in range(4):
                at = (h * 4 + ab) * 4 + k
                rows_ref[at : at + 1, :] = result[h * 4 + k][ab : ab + 1, :]
    sent = rows_ref[0:32, :].astype(BF16)
    for peer in range(16):
        out_ref[peer] = sent


def turn_kernel(in_ref, out_ref, rows_ref):
    for peer in range(16):
        part = in_ref[peer].astype(F32)
        for hab in range(8):
            at = hab * 64 + peer * 4
            rows_ref[at : at + 4, :] = part[hab * 4 : hab * 4 + 4, :]
    turned = rows_ref[...].T
    kept = jnp.concatenate([turned[0:40], turned[64:104]], axis=0).astype(BF16)
    for copy in range(8):
        out_ref[copy] = kept


def shifted_codes(codes, z_ref):
    lane = iota((1, LANES), 1)
    t, p = (lane >> 3) & 3, lane & 7
    for index, (h, a, b) in enumerate(COMBOS):
        by = 32 * b + 8 * h + a
        moved = pltpu.roll(codes, by, 1) if by else codes
        kept = jnp.where((t >= h) & (p >= a), moved, 0.0)
        z_ref[index * 64 : index * 64 + 64, :] = kept.astype(BF16)


def partial_adjoint(b_ref, bt_ref, x_ref, east_ref, west_ref, z_ref, r_ref, u_ref):
    for chunk in range(5):
        lanes = slice(chunk * 256, chunk * 256 + 256)
        z = z_ref[:, lanes]
        for u_lo in range(2):
            rows = slice(u_lo * HALF, u_lo * HALF + HALF)
            held = slice(u_lo * PACK, u_lo * PACK + HALF)
            if chunk < 4:
                x = x_ref[held, lanes]
            else:
                x = jnp.concatenate([east_ref[held, :], west_ref[held, :]], axis=1)
            r_ref[rows, :] = (dot(b_ref[rows, :], z) - x.astype(F32)).astype(BF16)
        u_ref[:, lanes] = dot(bt_ref[...], r_ref[...])
    lane = iota((1, LANES), 1)
    t, p = (lane >> 3) & 3, lane & 7
    total = u_ref[0:64, :]
    for index, (h, a, b) in enumerate(COMBOS[1:], 1):
        moved = pltpu.roll(u_ref[index * 64 : index * 64 + 64, :], LANES - (32 * b + 8 * h + a), 1)
        total = total + jnp.where((t < 4 - h) & (p < 8 - a), moved, 0.0)
    return total


def first_kernel(b_in, x_ref, east_ref, west_ref, sum_ref, y_ref, bt_ref, b_ref, z_ref, r_ref, u_ref):
    for j in range(8):
        b_ref[j * 80 : j * 80 + 80, :] = b_in[j]
    bt_ref[...] = b_ref[...].T

    def rows_of(start, count):
        part = slice(start, start + count)
        return jnp.concatenate([x_ref[part, :], east_ref[part, :], west_ref[part, :]], axis=1).astype(F32)

    high = rows_of(HALF, 64)
    middle = jnp.concatenate([rows_of(HALF + 64, 32), rows_of(PACK + HALF, 32)], axis=0)
    low = rows_of(PACK + HALF + 32, 64)
    codes = (high + middle) + low
    y_ref[...] = codes
    shifted_codes(codes, z_ref)
    sum_ref[...] = partial_adjoint(b_ref, bt_ref, x_ref, east_ref, west_ref, z_ref, r_ref, u_ref)


def shrunk(moving, gradient, shrink):
    descent = moving - STEP_SIZE * gradient
    size = jnp.maximum(jnp.abs(descent) - shrink, 0.0)
    return jnp.where(descent < 0.0, -size, size)


def middle_kernel(factor, mine_ref, other_ref, moving_ref, current_ref, limit_ref, bt_ref, b_in, x_ref, east_ref, west_ref, sum_ref, y_ref, now_ref, b_ref, z_ref, r_ref, u_ref):
    for j in range(8):
        b_ref[j * 80 : j * 80 + 80, :] = b_in[j]
    updated = shrunk(moving_ref[...], mine_ref[...] + other_ref[...], STEP_SIZE * limit_ref[...])
    moving = updated + factor * (updated - current_ref[...])
    now_ref[...] = updated
    y_ref[...] = moving
    shifted_codes(moving, z_ref)
    sum_ref[...] = partial_adjoint(b_ref, bt_ref, x_ref, east_ref, west_ref, z_ref, r_ref, u_ref)


def last_kernel(scale, place_ref, mine_ref, other_ref, moving_ref, limit_ref, b_in, x_ref, codes_ref, grad_ref, z_ref):
    codes = shrunk(moving_ref[...], mine_ref[...] + other_ref[...], STEP_SIZE * limit_ref[...])
    core, z, t = place_ref[0], place_ref[1], place_ref[2]
    own = iota((MAIN, 128), 1)
    source = (own & 31) * 32 + t * 8 + (2 * z + core) * 2 + ((own >> 5) & 1)
    order = onehot((iota((MAIN, 128), 0) == source) & (own < 64))
    high, middle, low = three(codes[:, 0:MAIN])
    codes_ref[...] = (dot(high, order) + dot(middle, order)) + dot(low, order)
    shifted_codes(codes, z_ref)
    z_main = z_ref[:, 0:MAIN]
    x = x_ref[pl.ds(pl.multiple_of(z * PACK + t * 80, 16), 80), :]
    residual = (dot(b_in[z * 4 + t], z_main) - x.astype(F32)).astype(BF16)
    filled = jnp.concatenate([residual, jnp.zeros((48, MAIN), BF16)], axis=0)
    grad = dot_t(z_main, filled) * scale
    for peer in range(16):
        for hab in range(8):
            at = hab * 64 + peer * 4
            grad_ref[peer, hab * 4 : hab * 4 + 4, :] = grad[at : at + 4, :]


def add_kernel(in_ref, out_ref):
    total = in_ref[0]
    for peer in range(1, 16):
        total = total + in_ref[peer]
    for copy in range(16):
        out_ref[copy] = total


def place_kernel(in_ref, out_ref, rows_ref):
    for k in range(4):
        for h in range(2):
            for ab in range(4):
                a, b = ab // 2, ab % 2
                for z in range(2):
                    for core in range(2):
                        for t in range(4):
                            at = a * 32 + (2 * core + z) * 8 + b * 4 + t
                            row = (h * 4 + ab) * 4 + k
                            rows_ref[at : at + 1, :] = in_ref[(2 * z + core) * 4 + t, row : row + 1, :]
            even = rows_ref[...]
            odd = pltpu.roll(even, 88, 1)
            turned = jnp.concatenate([even, odd], axis=0).T
            for i in range(39):
                lanes = slice((h * 39 + i) * 128, (h * 39 + i) * 128 + 128)
                out_ref[k : k + 1, lanes] = turned[i : i + 1, :]


def body(signal, dictionary, codes_init, thresholds):
    lat, tm = lax.axis_index("lat"), lax.axis_index("tm")
    z, core = lat // 2, lat % 2
    place = jnp.stack([core, z, tm]).astype(jnp.int32)
    lon = lax.axis_size("lon")
    same_core = [[(2 * i + c) * 4 + t for i in range(2) for t in range(4)] for c in range(2)]

    sliced = call(slice_kernel, [((16, 32, 128), BF16)], "dict_slice", [pltpu.VMEM((512, 128), F32)], 1, 2)(
        jnp.stack([2 * core + z, tm]).astype(jnp.int32), dictionary
    )
    rows = signal[0].reshape(39, 2, 8, 128).transpose(2, 1, 0, 3)
    rows = jnp.pad(rows, ((0, 0), (0, 0), (0, 1), (0, 0))).reshape(8, 80, 128)
    packed = call(pack_kernel, [((16, PACK, 128), BF16)], "pack", n_in=2)(rows, codes_init[0].reshape(64, 64))
    arrived = lax.all_to_all(packed, GROUP, 0, 0, tiled=True)
    sliced = lax.all_to_all(sliced, "lon", 0, 0, tiled=True)
    turned = call(turn_kernel, [((8, 80, 512), BF16)], "dict_turn", [pltpu.VMEM((512, 128), F32)])(sliced)
    blocks = lax.all_to_all(turned, GROUP, 0, 0, tiled=True, axis_index_groups=same_core)
    x, first, last = call(
        unpack_kernel,
        [((2 * PACK, MAIN), BF16), ((2 * PACK, 128), BF16), ((2 * PACK, 128), BF16)],
        "unpack",
        [pltpu.VMEM((2 * PACK, MAIN), BF16)],
    )(arrived)
    east = lax.ppermute(first, "lon", [(i, (i - 1) % lon) for i in range(lon)])
    west = lax.ppermute(last, "lon", [(i, (i + 1) % lon) for i in range(lon)])

    work = [
        pltpu.VMEM((640, 512), BF16),
        pltpu.VMEM((512, LANES), BF16),
        pltpu.VMEM((640, 256), BF16),
        pltpu.VMEM((512, LANES), F32),
    ]
    state = ((64, LANES), F32)
    limits = thresholds.reshape(64, 1)
    mine, moving, blocks_t = call(
        first_kernel, [state, state, ((512, 640), BF16)], "first", work, n_in=4
    )(blocks, x, east, west)
    swap = [(i, i ^ 1) for i in range(4)]
    current = moving
    momentum_now = 1.0
    for turn in range(ITERS - 1):
        other = lax.ppermute(mine, "lat", swap)
        momentum_next = (1.0 + math.sqrt(1.0 + 4.0 * momentum_now * momentum_now)) / 2.0
        factor = (momentum_now - 1.0) / momentum_next
        momentum_now = momentum_next

        def step(*refs):
            middle_kernel(factor, *refs)

        mine, moving, current = call(step, [state, state, state], "middle", work, n_in=10)(
            mine, other, moving, current, limits, blocks_t, blocks, x, east, west
        )
    other = lax.ppermute(mine, "lat", swap)
    positions = lax.axis_size("tm") * lax.axis_size("lat") * lon * 64

    def ending(*refs):
        last_kernel(1.0 / math.sqrt(positions), *refs)

    codes, grad = call(
        ending, [((64, 128), F32), ((16, 32, 128), F32)], "last", [pltpu.VMEM((512, LANES), BF16)], 1, 7
    )(place, mine, other, moving, limits, blocks, x)
    grad = lax.all_to_all(grad, "lon", 0, 0, tiled=True)
    summed = call(add_kernel, [((16, 32, 128), F32)], "add")(grad)
    summed = lax.all_to_all(summed, GROUP, 0, 0, tiled=True)
    gradient = call(place_kernel, [((4, 9984), F32)], "place", [pltpu.VMEM((64, 128), F32)])(summed)
    return codes[:, :64].reshape(1, 64, 2, 32), gradient


def solution(mesh):
    placed = (P("tm", None, "lat", "lon"), P("lon", None), P("tm", None, "lat", "lon"), P())
    return jax.shard_map(
        body,
        mesh=mesh,
        in_specs=placed,
        out_specs=(P("tm", None, "lat", "lon"), P("lon", None)),
        check_vma=False,
    )
```

```python
import math

import jax
import jax.numpy as jnp
from jax import lax
from jax.experimental import pallas as pl
from jax.experimental.pallas import tpu as pltpu
from jax.sharding import PartitionSpec as P


ITERS = 2
STEP_SIZE = 0.5
F32 = jnp.float32
BF16 = jnp.bfloat16
GROUP = ("lat", "tm")
COMBOS = [(h, a, b) for h in (0, 1) for a in (0, 1) for b in (0, 1)]
MAIN = 1024
LANES = 1280
HALF = 320
PACK = 384


def iota(shape, dim):
    return lax.broadcasted_iota(jnp.int32, shape, dim)


def dot(a, b):
    return jnp.dot(a, b, preferred_element_type=F32)


def dot_t(a, b):
    return lax.dot_general(a, b, (((1,), (1,)), ((), ())), preferred_element_type=F32)


def onehot(test):
    return jnp.where(test, 1.0, 0.0).astype(BF16)


def two(x):
    high = x.astype(BF16)
    return high, (x - high.astype(F32)).astype(BF16)


def three(x):
    high = x.astype(BF16)
    rest = x - high.astype(F32)
    middle = rest.astype(BF16)
    return high, middle, (rest - middle.astype(F32)).astype(BF16)


def call(kernel, outs, scratch=(), smem=0, n_in=1):
    vmem = pl.BlockSpec(memory_space=pltpu.VMEM)
    specs = [pl.BlockSpec(memory_space=pltpu.SMEM)] * smem + [vmem] * (n_in - smem)
    shapes = [jax.ShapeDtypeStruct(s, d) for s, d in outs]
    return pl.pallas_call(
        kernel,
        out_shape=shapes if len(shapes) > 1 else shapes[0],
        in_specs=specs,
        out_specs=[vmem] * len(shapes) if len(shapes) > 1 else vmem,
        scratch_shapes=list(scratch),
        compiler_params=pltpu.CompilerParams(vmem_limit_bytes=48 * 1024 * 1024),
    )


def pack_kernel(place_ref, x_ref, z_ref, own_ref, other_ref):
    row, col = iota((128, 128), 0), iota((128, 128), 1)
    order = onehot(((row & 3) * 32 + (row >> 2)) == col)
    lane = iota((80, 128), 1)
    high, low = two(z_ref[...])
    codes = jnp.concatenate([high, low], axis=1)
    for flip, out_ref in enumerate((own_ref, other_ref)):
        first = (place_ref[0] ^ flip) * 2
        split = [dot(x_ref[p2 * 4 + first + u_lo], order) for u_lo in range(2) for p2 in range(2)]
        for v in range(4):
            piece = jnp.zeros((80, 128), F32)
            for slot in range(4):
                by = ((slot - v) % 4) * 32
                moved = pltpu.roll(split[slot], by, 1) if by else split[slot]
                piece = jnp.where((lane >> 5) == slot, moved, piece)
            out_ref[v * 80 : v * 80 + 80, :] = piece.astype(BF16)
        out_ref[HALF:PACK, :] = codes


def unpack_kernel(place_ref, *refs):
    hours, (main_ref, first_ref, last_ref, left_ref) = refs[:4], refs[4:]
    lane = iota((PACK, 128), 1)
    for pair in range(8):
        even = hours[pair // 2][2 * (pair % 2)].astype(F32)
        odd = hours[pair // 2][2 * (pair % 2) + 1].astype(F32)
        lanes = slice(pair * 128, pair * 128 + 128)
        left_ref[0:PACK, lanes] = jnp.where(lane < 64, even, pltpu.roll(odd, 64, 1)).astype(BF16)
        left_ref[PACK : 2 * PACK, lanes] = jnp.where(lane < 64, pltpu.roll(even, 64, 1), odd).astype(BF16)
    lat, hour = 2 * place_ref[1] + place_ref[0], place_ref[2]
    for block in range(4):
        n = iota((1024, 256), 1) + block * 256
        slab = (((n >> 3) & 3) ^ hour) * 4 + (((n >> 1) & 3) ^ lat)
        source = slab * 64 + (n & 1) * 32 + (n >> 5)
        order = onehot(iota((1024, 256), 0) == source)
        main_ref[:, block * 256 : block * 256 + 256] = dot(left_ref[...], order).astype(BF16)
    first_ref[...] = main_ref[:, 0:128]
    last_ref[...] = main_ref[:, MAIN - 128 : MAIN]


def slice_kernel(place_ref, d_ref, out_ref, rows_ref):
    rows_ref[...] = jnp.zeros((512, 128), F32)
    for i in range(78):
        h, half = i // 39, i % 39
        part = d_ref[:, i * 128 : i * 128 + 128].astype(F32)
        for k in range(4):
            at = (k * 2 + h) * 64 + half
            rows_ref[at : at + 1, :] = part[k : k + 1, :]
    u, v = place_ref[0], place_ref[1]
    which = iota((8, 128), 0)
    want = (which >> 2) * 64 + ((which >> 1) & 1) * 32 + u * 8 + (which & 1) * 4 + v
    picked = dot_t(onehot(iota((8, 128), 1) == want), rows_ref[...].astype(BF16))
    lane = iota((4, 128), 1)
    result = [None] * 8
    for k in range(4):
        pair = picked[:, k * 128 : k * 128 + 128]
        turned = pltpu.roll(pair, 64, 1)
        result[k] = jnp.where(lane < 64, pair[0:4], turned[4:8])
        result[4 + k] = jnp.where(lane < 64, turned[0:4], pair[4:8])
    for h in range(2):
        for ab in range(4):
            for k in range(4):
                at = (h * 4 + ab) * 4 + k
                rows_ref[at : at + 1, :] = result[h * 4 + k][ab : ab + 1, :]
    sent = rows_ref[0:32, :].astype(BF16)
    for peer in range(16):
        out_ref[peer] = sent


def turn_kernel(in_ref, out_ref, rows_ref):
    for peer in range(16):
        part = in_ref[peer].astype(F32)
        for hab in range(8):
            at = hab * 64 + peer * 4
            rows_ref[at : at + 4, :] = part[hab * 4 : hab * 4 + 4, :]
    turned = rows_ref[...].T
    kept = jnp.concatenate([turned[0:40], turned[64:104]], axis=0).astype(BF16)
    for copy in range(8):
        out_ref[copy * 80 : copy * 80 + 80, :] = kept


def shifted_codes(codes, z_ref):
    lane = iota((1, LANES), 1)
    t, p = (lane >> 3) & 3, lane & 7
    for index, (h, a, b) in enumerate(COMBOS):
        by = 32 * b + 8 * h + a
        moved = pltpu.roll(codes, by, 1) if by else codes
        kept = jnp.where((t >= h) & (p >= a), moved, 0.0)
        z_ref[index * 64 : index * 64 + 64, :] = kept.astype(BF16)


def partial_adjoint(b_ref, bt_ref, x_ref, east_ref, west_ref, z_ref, r_ref, u_ref):
    for chunk in range(5):
        lanes = slice(chunk * 256, chunk * 256 + 256)
        z = z_ref[:, lanes]
        for u_lo in range(2):
            rows = slice(u_lo * HALF, u_lo * HALF + HALF)
            held = slice(u_lo * PACK, u_lo * PACK + HALF)
            if chunk < 4:
                x = x_ref[held, lanes]
            else:
                x = jnp.concatenate([east_ref[held, :], west_ref[held, :]], axis=1)
            r_ref[rows, :] = (dot(b_ref[rows, :], z) - x.astype(F32)).astype(BF16)
        u_ref[:, lanes] = dot(bt_ref[...], r_ref[...])
    lane = iota((1, LANES), 1)
    t, p = (lane >> 3) & 3, lane & 7
    total = u_ref[0:64, :]
    for index, (h, a, b) in enumerate(COMBOS[1:], 1):
        moved = pltpu.roll(u_ref[index * 64 : index * 64 + 64, :], LANES - (32 * b + 8 * h + a), 1)
        total = total + jnp.where((t < 4 - h) & (p < 8 - a), moved, 0.0)
    return total


def first_kernel(b_ref, x_ref, east_ref, west_ref, sum_ref, y_ref, bt_ref, z_ref, r_ref, u_ref):
    bt_ref[...] = b_ref[...].T

    def rows_of(start, count):
        part = slice(start, start + count)
        return jnp.concatenate([x_ref[part, :], east_ref[part, :], west_ref[part, :]], axis=1).astype(F32)

    codes = rows_of(HALF, 64) + rows_of(PACK + HALF, 64)
    y_ref[...] = codes
    shifted_codes(codes, z_ref)
    sum_ref[...] = partial_adjoint(b_ref, bt_ref, x_ref, east_ref, west_ref, z_ref, r_ref, u_ref)


def shrunk(moving, gradient, shrink):
    descent = moving - STEP_SIZE * gradient
    size = jnp.maximum(jnp.abs(descent) - shrink, 0.0)
    return jnp.where(descent < 0.0, -size, size)


def middle_kernel(factor, mine_ref, other_ref, moving_ref, current_ref, limit_ref, bt_ref, b_ref, x_ref, east_ref, west_ref, sum_ref, y_ref, now_ref, z_ref, r_ref, u_ref):
    updated = shrunk(moving_ref[...], mine_ref[...] + other_ref[...], STEP_SIZE * limit_ref[...])
    moving = updated + factor * (updated - current_ref[...])
    now_ref[...] = updated
    y_ref[...] = moving
    shifted_codes(moving, z_ref)
    sum_ref[...] = partial_adjoint(b_ref, bt_ref, x_ref, east_ref, west_ref, z_ref, r_ref, u_ref)


def last_kernel(scale, place_ref, mine_ref, other_ref, moving_ref, limit_ref, b_ref, x_ref, codes_ref, grad_ref, z_ref, g_ref):
    codes = shrunk(moving_ref[...], mine_ref[...] + other_ref[...], STEP_SIZE * limit_ref[...])
    core, z, t = place_ref[0], place_ref[1], place_ref[2]
    own = iota((MAIN, 128), 1)
    source = (own & 31) * 32 + t * 8 + (2 * z + core) * 2 + ((own >> 5) & 1)
    order = onehot((iota((MAIN, 128), 0) == source) & (own < 64))
    high, middle, low = three(codes[:, 0:MAIN])
    codes_ref[...] = (dot(high, order) + dot(middle, order)) + dot(low, order)
    shifted_codes(codes, z_ref)
    z_main = z_ref[:, 0:MAIN]
    x = x_ref[pl.ds(pl.multiple_of(z * PACK, 16), HALF), :]
    held = b_ref[pl.ds(pl.multiple_of(z * HALF, 16), HALF), :]
    residual = (dot(held, z_main) - x.astype(F32)).astype(BF16)
    g_ref[...] = dot_t(z_main, residual) * scale
    for peer in range(16):
        parts = [g_ref[hab * 64 + peer * 4 : hab * 64 + peer * 4 + 4, :] for hab in range(8)]
        grad_ref[peer] = jnp.concatenate(parts, axis=0).astype(BF16)


def add_kernel(in_ref, out_ref):
    total = in_ref[0].astype(F32)
    for peer in range(1, 16):
        total = total + in_ref[peer].astype(F32)
    out_ref[...] = total


def place_kernel(place_ref, own_ref, core_ref, z_ref, both_ref, out_ref, parts_ref, rows_ref):
    core, z = place_ref[0], place_ref[1]
    for flip, piece in enumerate((own_ref, core_ref, z_ref, both_ref)):
        u = 2 * (core ^ (flip & 1)) + (z ^ (flip >> 1))
        for v in range(4):
            low = v * 80 // 128 * 128
            turn = v * 80 - low
            lanes = piece[:, low : min(low + 256, HALF)]
            if lanes.shape[1] < 256:
                lanes = jnp.concatenate([lanes, jnp.zeros((32, 256 - lanes.shape[1]), F32)], axis=1)
            moved = pltpu.roll(lanes, 256 - turn, 1) if turn else lanes
            parts_ref[u * 4 + v] = moved[:, 0:128]
    for k in range(4):
        for h in range(2):
            for ab in range(4):
                row = (h * 4 + ab) * 4 + k
                for uv in range(16):
                    at = (ab // 2) * 32 + (uv // 4) * 8 + (ab % 2) * 4 + uv % 4
                    rows_ref[at : at + 1, :] = parts_ref[uv, row : row + 1, :]
            even = rows_ref[...]
            odd = pltpu.roll(even, 88, 1)
            turned = jnp.concatenate([even, odd], axis=0).T
            for i in range(39):
                lanes = slice((h * 39 + i) * 128, (h * 39 + i) * 128 + 128)
                out_ref[k : k + 1, lanes] = turned[i : i + 1, :]


def program(signal, dictionary, codes_init, thresholds):
    lat, tm = lax.axis_index("lat"), lax.axis_index("tm")
    z, core = lat // 2, lat % 2
    place = jnp.stack([core, z, tm]).astype(jnp.int32)
    lon = lax.axis_size("lon")
    same_core = [[(2 * i + c) * 4 + t for i in range(2) for t in range(4)] for c in range(2)]

    sliced = call(slice_kernel, [((16, 32, 128), BF16)], [pltpu.VMEM((512, 128), F32)], 1, 2)(
        jnp.stack([2 * core + z, tm]).astype(jnp.int32), dictionary
    )
    rows = signal[0].reshape(39, 2, 8, 128).transpose(2, 1, 0, 3)
    rows = jnp.pad(rows, ((0, 0), (0, 0), (0, 1), (0, 0))).reshape(8, 80, 128)
    kept, given = call(pack_kernel, [((PACK, 128), BF16)] * 2, (), 1, 3)(
        place, rows, codes_init[0].reshape(64, 64)
    )

    def flipped(block, axis, by):
        return lax.ppermute(block, axis, [(i, i ^ by) for i in range(4)])

    beside = flipped(given, "lat", 1)
    bands = [kept, beside, flipped(kept, "lat", 2), flipped(beside, "lat", 2)]
    hour = jnp.stack(bands)
    hours = [hour] + [flipped(hour, "tm", by) for by in (1, 2, 3)]
    sliced = lax.all_to_all(sliced, "lon", 0, 0, tiled=True)
    turned = call(turn_kernel, [((640, 512), BF16)], [pltpu.VMEM((512, 128), F32)])(sliced)
    blocks = lax.all_to_all(turned, GROUP, 0, 0, tiled=True, axis_index_groups=same_core)
    x, first, last = call(
        unpack_kernel,
        [((2 * PACK, MAIN), BF16), ((2 * PACK, 128), BF16), ((2 * PACK, 128), BF16)],
        [pltpu.VMEM((2 * PACK, MAIN), BF16)],
        1,
        5,
    )(place, *hours)
    east = lax.ppermute(first, "lon", [(i, (i - 1) % lon) for i in range(lon)])
    west = lax.ppermute(last, "lon", [(i, (i + 1) % lon) for i in range(lon)])

    work = [
        pltpu.VMEM((512, LANES), BF16),
        pltpu.VMEM((640, 256), BF16),
        pltpu.VMEM((512, LANES), F32),
    ]
    state = ((64, LANES), F32)
    limits = thresholds.reshape(64, 1)
    mine, moving, blocks_t = call(
        first_kernel, [state, state, ((512, 640), BF16)], work, n_in=4
    )(blocks, x, east, west)
    swap = [(i, i ^ 1) for i in range(4)]
    current = moving
    momentum_now = 1.0
    for _ in range(ITERS - 1):
        other = lax.ppermute(mine, "lat", swap)
        momentum_next = (1.0 + math.sqrt(1.0 + 4.0 * momentum_now * momentum_now)) / 2.0
        factor = (momentum_now - 1.0) / momentum_next
        momentum_now = momentum_next

        def step(*refs):
            middle_kernel(factor, *refs)

        mine, moving, current = call(step, [state, state, state], work, n_in=10)(
            mine, other, moving, current, limits, blocks_t, blocks, x, east, west
        )
    other = lax.ppermute(mine, "lat", swap)
    positions = lax.axis_size("tm") * lax.axis_size("lat") * lon * 64

    def ending(*refs):
        last_kernel(1.0 / math.sqrt(positions), *refs)

    codes, grad = call(
        ending,
        [((64, 128), F32), ((16, 32, HALF), BF16)],
        [pltpu.VMEM((512, LANES), BF16), pltpu.VMEM((512, HALF), F32)],
        1,
        7,
    )(place, mine, other, moving, limits, blocks, x)
    grad = lax.all_to_all(grad, "lon", 0, 0, tiled=True)
    summed = call(add_kernel, [((32, HALF), F32)])(grad)
    others = [lax.ppermute(summed, "lat", [(i, i ^ flip) for i in range(4)]) for flip in (1, 2, 3)]
    gradient = call(
        place_kernel,
        [((4, 9984), F32)],
        [pltpu.VMEM((16, 32, 128), F32), pltpu.VMEM((64, 128), F32)],
        1,
        5,
    )(place, summed, *others)
    return codes[:, :64].reshape(1, 64, 2, 32), gradient


def solution(mesh):
    placed = (P("tm", None, "lat", "lon"), P("lon", None), P("tm", None, "lat", "lon"), P())
    return jax.shard_map(
        program,
        mesh=mesh,
        in_specs=placed,
        out_specs=(P("tm", None, "lat", "lon"), P("lon", None)),
        check_vma=False,
    )
```

```python
import math

import jax
import jax.numpy as jnp
from jax import lax
from jax.experimental import pallas as pl
from jax.experimental.pallas import tpu as pltpu
from jax.sharding import PartitionSpec as P


ITERS = 2
STEP_SIZE = 0.5
F32 = jnp.float32
BF16 = jnp.bfloat16
COMBOS = [(h, a, b) for h in (0, 1) for a in (0, 1) for b in (0, 1)]
MAIN = 1024
LANES = 1280
HALF = 320
PACK = 384
SIDE = 96


def iota(shape, dim):
    return lax.broadcasted_iota(jnp.int32, shape, dim)


def dot(a, b):
    return jnp.dot(a, b, preferred_element_type=F32)


def dot_t(a, b):
    return lax.dot_general(a, b, (((1,), (1,)), ((), ())), preferred_element_type=F32)


def onehot(test):
    return jnp.where(test, 1.0, 0.0).astype(BF16)


def two(x):
    high = x.astype(BF16)
    return high, (x - high.astype(F32)).astype(BF16)


def three(x):
    high = x.astype(BF16)
    rest = x - high.astype(F32)
    middle = rest.astype(BF16)
    return high, middle, (rest - middle.astype(F32)).astype(BF16)


def call(kernel, outs, scratch=(), smem=0, n_in=1, space=pltpu.VMEM):
    vmem = pl.BlockSpec(memory_space=pltpu.VMEM)
    held = pl.BlockSpec(memory_space=space)
    specs = [pl.BlockSpec(memory_space=pltpu.SMEM)] * smem + [held] * (n_in - smem)
    shapes = [jax.ShapeDtypeStruct(s, d) for s, d in outs]
    return pl.pallas_call(
        kernel,
        out_shape=shapes if len(shapes) > 1 else shapes[0],
        in_specs=specs,
        out_specs=[vmem] * len(shapes) if len(shapes) > 1 else vmem,
        scratch_shapes=list(scratch),
        compiler_params=pltpu.CompilerParams(vmem_limit_bytes=16 * 1024 * 1024),
    )


def edge_kernel(x_ref, z_ref, west_ref, east_ref):
    high, low = two(z_ref[...])
    codes = jnp.concatenate([high, low], axis=0)
    row, col = iota((128, 128), 0), iota((128, 128), 1)
    for first, out_ref in ((0, west_ref), (28, east_ref)):
        total = jnp.zeros((80, 128), F32)
        wanted = (first + (col & 3)) * 4 + ((col >> 3) & 3)
        for r in range(8):
            pick = (row == wanted) & ((col >> 5) == r % 4) & (((col >> 2) & 1) == r // 4)
            total = total + dot(x_ref[r], onehot(pick))
        out_ref[0:80, :] = total.astype(BF16)
        lane = iota((64, 128), 1)
        pick = (lane < 8) & (iota((64, 128), 0) == (lane >> 2) * 32 + first + (lane & 3))
        narrow = dot(codes, onehot(pick))
        edge = narrow[0:8]
        for group in range(1, 16):
            edge = edge + pltpu.roll(narrow[group * 8 : group * 8 + 8], group * 8, 1)
        out_ref[80:96, :] = jnp.concatenate([edge, jnp.zeros((8, 128), F32)], axis=0).astype(BF16)


def pack_kernel(place_ref, x_ref, z_ref, own_ref, other_ref):
    row, col = iota((128, 128), 0), iota((128, 128), 1)
    order = onehot(((row & 3) * 32 + (row >> 2)) == col)
    lane = iota((80, 128), 1)
    high, low = two(z_ref[...])
    codes = jnp.concatenate([high, low], axis=1)
    for flip, out_ref in enumerate((own_ref, other_ref)):
        first = (place_ref[0] ^ flip) * 2
        split = [dot(x_ref[p2 * 4 + first + u_lo], order) for u_lo in range(2) for p2 in range(2)]
        for v in range(4):
            piece = jnp.zeros((80, 128), F32)
            for slot in range(4):
                by = ((slot - v) % 4) * 32
                moved = pltpu.roll(split[slot], by, 1) if by else split[slot]
                piece = jnp.where((lane >> 5) == slot, moved, piece)
            out_ref[v * 80 : v * 80 + 80, :] = piece.astype(BF16)
        out_ref[HALF:PACK, :] = codes


def side_kernel(place_ref, east_ref, west_ref, own_ref, other_ref):
    row, col = iota((128, 128), 0), iota((128, 128), 1)
    is_east = (col & 7) < 4
    within = ((col >> 3) & 1) * 4 + (col & 3)
    sides = []
    for part in range(2):
        pick = row == (2 * (col >> 4) + part) * 8 + within
        east = dot(east_ref[80:96, :], onehot(pick & is_east))
        west = dot(west_ref[80:96, :], onehot(pick & jnp.logical_not(is_east)))
        sides.append((east + west)[0:8])
    codes = jnp.concatenate(sides, axis=0).astype(BF16)
    for flip, out_ref in enumerate((own_ref, other_ref)):
        pick = row == ((place_ref[0] ^ flip) * 8 + (col >> 4)) * 8 + within
        east = dot(east_ref[0:80, :], onehot(pick & is_east))
        west = dot(west_ref[0:80, :], onehot(pick & jnp.logical_not(is_east)))
        out_ref[0:80, :] = (east + west).astype(BF16)
        out_ref[80:SIDE, :] = codes


def unpack_kernel(place_ref, *refs):
    main_ref, edge_ref, left_ref, side_ref, hours, edges, arrived = refs[8:]
    copies = [
        pltpu.make_async_copy(refs[i], hours.at[i] if i < 4 else edges.at[i - 4], arrived.at[i]) for i in range(8)
    ]
    for copy in copies:
        copy.start()
    lane = iota((PACK, 128), 1)
    for pair in range(8):
        if pair % 2 == 0:
            copies[pair // 2].wait()
        even = hours[pair // 2, 2 * (pair % 2)].astype(F32)
        odd = hours[pair // 2, 2 * (pair % 2) + 1].astype(F32)
        lanes = slice(pair * 128, pair * 128 + 128)
        left_ref[0:PACK, lanes] = jnp.where(lane < 64, even, pltpu.roll(odd, 64, 1)).astype(BF16)
        left_ref[PACK : 2 * PACK, lanes] = jnp.where(lane < 64, pltpu.roll(even, 64, 1), odd).astype(BF16)
    lat, hour = 2 * place_ref[1] + place_ref[0], place_ref[2]
    for block in range(4):
        n = iota((1024, 256), 1) + block * 256
        slab = (((n >> 3) & 3) ^ hour) * 4 + (((n >> 1) & 3) ^ lat)
        source = slab * 64 + (n & 1) * 32 + (n >> 5)
        order = onehot(iota((1024, 256), 0) == source)
        main_ref[:, block * 256 : block * 256 + 256] = dot(left_ref[...], order).astype(BF16)
    lane = iota((SIDE, 128), 1)
    for copy in copies[4:]:
        copy.wait()
    for half in range(2):
        slabs = [edges[half * 2 + s // 4, s % 4].astype(F32) for s in range(8)]
        for group in range(8):
            piece = jnp.zeros((SIDE, 128), F32)
            for s in range(8):
                by = ((s - group) % 8) * 16
                moved = pltpu.roll(slabs[s], by, 1) if by else slabs[s]
                piece = jnp.where((lane >> 4) == s, moved, piece)
            side_ref[group * 96 : group * 96 + 96, half * 128 : half * 128 + 128] = piece.astype(BF16)
    n = iota((256, 256), 1)
    slab = (((n >> 3) & 3) ^ hour) * 4 + (((n >> 1) & 3) ^ lat)
    order = onehot(iota((256, 256), 0) == slab * 16 + (n & 1) * 8 + (n >> 5))
    sides = dot(side_ref[...], order).astype(BF16)
    for group in range(8):
        at = (group // 4) * PACK + (group % 4) * 80
        edge_ref[at : at + 80, :] = sides[group * 96 : group * 96 + 80]
        at = (group // 4) * PACK + HALF + (group % 4) * 16
        edge_ref[at : at + 16, :] = sides[group * 96 + 80 : group * 96 + 96]


def slice_kernel(place_ref, d_ref, out_ref, rows_ref):
    rows_ref[...] = jnp.zeros((512, 128), F32)
    for i in range(78):
        h, half = i // 39, i % 39
        part = d_ref[:, i * 128 : i * 128 + 128].astype(F32)
        for k in range(4):
            at = (k * 2 + h) * 64 + half
            rows_ref[at : at + 1, :] = part[k : k + 1, :]
    which = iota((32, 128), 0)
    want = ((which >> 2) & 1) * 64 + ((which >> 1) & 1) * 32 + place_ref[0] * 8 + (which & 1) * 4 + (which >> 3)
    picked = dot_t(onehot(iota((32, 128), 1) == want), rows_ref[...].astype(BF16))
    lane = iota((4, 128), 1)
    for v in range(4):
        for k in range(4):
            pair = picked[v * 8 : v * 8 + 8, k * 128 : k * 128 + 128]
            turned = pltpu.roll(pair, 64, 1)
            even = jnp.where(lane < 64, pair[0:4], turned[4:8])
            odd = jnp.where(lane < 64, turned[0:4], pair[4:8])
            for ab in range(4):
                at = v * 32 + ab * 4 + k
                rows_ref[at : at + 1, :] = even[ab : ab + 1, :]
                rows_ref[at + 16 : at + 17, :] = odd[ab : ab + 1, :]
    sent = rows_ref[0:128, :].astype(BF16)
    for peer in range(16):
        out_ref[peer] = sent


def turn_kernel(in_ref, out_ref, rows_ref):
    for v in range(4):
        for peer in range(16):
            part = in_ref[peer, v * 32 : v * 32 + 32].astype(F32)
            for hab in range(8):
                at = hab * 64 + peer * 4
                rows_ref[v, at : at + 4, :] = part[hab * 4 : hab * 4 + 4, :]
        turned = rows_ref[v].T
        kept = jnp.concatenate([turned[0:40], turned[64:104]], axis=0)
        out_ref[v * 80 : v * 80 + 80, :] = kept.astype(BF16)


def shifted_codes(codes, z_ref):
    lane = iota((1, LANES), 1)
    t, p = (lane >> 3) & 3, lane & 7
    for index, (h, a, b) in enumerate(COMBOS):
        by = 32 * b + 8 * h + a
        moved = pltpu.roll(codes, by, 1) if by else codes
        kept = jnp.where((t >= h) & (p >= a), moved, 0.0)
        z_ref[index * 64 : index * 64 + 64, :] = kept.astype(BF16)


def partial_adjoint(z, b_ref, bt_ref, x_ref, edge_ref, z_ref, r_ref, u_ref):
    for chunk in range(5):
        lanes = slice(chunk * 256, chunk * 256 + 256)
        codes = z_ref[:, lanes]
        for slot in range(2):
            rows = slice(slot * HALF, slot * HALF + HALF)
            held = pl.ds(pl.multiple_of((z ^ slot) * PACK, PACK), HALF)
            x = x_ref[held, lanes] if chunk < 4 else edge_ref[held, :]
            r_ref[rows, :] = (dot(b_ref[rows, :], codes) - x.astype(F32)).astype(BF16)
        u_ref[:, lanes] = dot(bt_ref[...], r_ref[...])
    lane = iota((1, LANES), 1)
    t, p = (lane >> 3) & 3, lane & 7
    total = u_ref[0:64, :]
    for index, (h, a, b) in enumerate(COMBOS[1:], 1):
        moved = pltpu.roll(u_ref[index * 64 : index * 64 + 64, :], LANES - (32 * b + 8 * h + a), 1)
        total = total + jnp.where((t < 4 - h) & (p < 8 - a), moved, 0.0)
    return total


def first_kernel(place_ref, own_ref, other_ref, x_ref, edge_ref, sum_ref, y_ref, b_ref, bt_ref, z_ref, r_ref, u_ref):
    b_ref[0:HALF, :] = own_ref[...]
    b_ref[HALF : 2 * HALF, :] = other_ref[...]
    bt_ref[...] = b_ref[...].T

    def rows_of(start, count):
        part = slice(start, start + count)
        return jnp.concatenate([x_ref[part, :], edge_ref[part, :]], axis=1).astype(F32)

    codes = rows_of(HALF, 64) + rows_of(PACK + HALF, 64)
    y_ref[...] = codes
    shifted_codes(codes, z_ref)
    sum_ref[...] = partial_adjoint(place_ref[1], b_ref, bt_ref, x_ref, edge_ref, z_ref, r_ref, u_ref)


def shrunk(moving, gradient, limits):
    same = iota((64, 64), 0) == iota((64, 64), 1)
    shrink = STEP_SIZE * jnp.sum(jnp.where(same, limits, 0.0), axis=1, keepdims=True)
    descent = moving - STEP_SIZE * gradient
    size = jnp.maximum(jnp.abs(descent) - shrink, 0.0)
    return jnp.where(descent < 0.0, -size, size)


def middle_kernel(factor, place_ref, mine_ref, other_ref, moving_ref, current_ref, limit_ref, bt_ref, b_ref, x_ref, edge_ref, sum_ref, y_ref, now_ref, z_ref, r_ref, u_ref):
    updated = shrunk(moving_ref[...], mine_ref[...] + other_ref[...], limit_ref[...])
    moving = updated + factor * (updated - current_ref[...])
    now_ref[...] = updated
    y_ref[...] = moving
    shifted_codes(moving, z_ref)
    sum_ref[...] = partial_adjoint(place_ref[1], b_ref, bt_ref, x_ref, edge_ref, z_ref, r_ref, u_ref)


def last_kernel(scale, place_ref, mine_ref, other_ref, moving_ref, limit_ref, b_ref, x_ref, codes_ref, grad_ref, z_ref, g_ref):
    codes = shrunk(moving_ref[...], mine_ref[...] + other_ref[...], limit_ref[...])
    core, z, t = place_ref[0], place_ref[1], place_ref[2]
    own = iota((MAIN, 128), 1)
    source = (own & 31) * 32 + t * 8 + (2 * z + core) * 2 + ((own >> 5) & 1)
    order = onehot((iota((MAIN, 128), 0) == source) & (own < 64))
    high, middle, low = three(codes[:, 0:MAIN])
    codes_ref[...] = (dot(high, order) + dot(middle, order)) + dot(low, order)
    shifted_codes(codes, z_ref)
    z_main = z_ref[:, 0:MAIN]
    x = x_ref[pl.ds(pl.multiple_of(z * PACK, 16), HALF), :]
    residual = (dot(b_ref[0:HALF, :], z_main) - x.astype(F32)).astype(BF16)
    g_ref[...] = dot_t(z_main, residual) * scale
    for peer in range(16):
        parts = [g_ref[hab * 64 + peer * 4 : hab * 64 + peer * 4 + 4, :] for hab in range(8)]
        grad_ref[peer] = jnp.concatenate(parts, axis=0).astype(BF16)


def add_kernel(in_ref, out_ref):
    total = in_ref[0].astype(F32)
    for peer in range(1, 16):
        total = total + in_ref[peer].astype(F32)
    out_ref[...] = total


def place_kernel(place_ref, own_ref, core_ref, z_ref, both_ref, out_ref, parts_ref, rows_ref):
    core, z = place_ref[0], place_ref[1]
    for flip, piece in enumerate((own_ref, core_ref, z_ref, both_ref)):
        u = 2 * (core ^ (flip & 1)) + (z ^ (flip >> 1))
        for v in range(4):
            low = v * 80 // 128 * 128
            turn = v * 80 - low
            lanes = piece[:, low : min(low + 256, HALF)]
            if lanes.shape[1] < 256:
                lanes = jnp.concatenate([lanes, jnp.zeros((32, 256 - lanes.shape[1]), F32)], axis=1)
            moved = pltpu.roll(lanes, 256 - turn, 1) if turn else lanes
            parts_ref[u * 4 + v] = moved[:, 0:128]
    for k in range(4):
        for h in range(2):
            for ab in range(4):
                row = (h * 4 + ab) * 4 + k
                for uv in range(16):
                    at = (ab // 2) * 32 + (uv // 4) * 8 + (ab % 2) * 4 + uv % 4
                    rows_ref[at : at + 1, :] = parts_ref[uv, row : row + 1, :]
            even = rows_ref[...]
            odd = pltpu.roll(even, 88, 1)
            turned = jnp.concatenate([even, odd], axis=0).T
            for i in range(39):
                lanes = slice((h * 39 + i) * 128, (h * 39 + i) * 128 + 128)
                out_ref[k : k + 1, lanes] = turned[i : i + 1, :]


def program(signal, dictionary, codes_init, thresholds):
    lat, tm = lax.axis_index("lat"), lax.axis_index("tm")
    z, core = lat // 2, lat % 2
    place = jnp.stack([core, z, tm]).astype(jnp.int32)
    lon = lax.axis_size("lon")

    ring = [[(i, (i + by) % lon) for i in range(lon)] for by in (-1, 1)]

    def flipped(block, axis, by):
        return lax.ppermute(block, axis, [(i, i ^ by) for i in range(4)])

    rows = signal[0].reshape(39, 2, 8, 128).transpose(2, 1, 0, 3)
    rows = jnp.pad(rows, ((0, 0), (0, 0), (0, 1), (0, 0))).reshape(8, 80, 128)
    start = codes_init[0].reshape(64, 64)

    def joined(kept, given):
        beside = flipped(given, "lat", 1)
        bands = [kept, beside, flipped(kept, "lat", 2), flipped(beside, "lat", 2)]
        hour = jnp.stack(bands)
        return [hour] + [flipped(hour, "tm", by) for by in (1, 2, 3)]

    west, east = call(edge_kernel, [((SIDE, 128), BF16)] * 2, n_in=2)(rows, start)
    east, west = lax.ppermute(west, "lon", ring[0]), lax.ppermute(east, "lon", ring[1])
    packed = call(pack_kernel, [((PACK, 128), BF16)] * 2, (), 1, 3)(place, rows, start)
    fields = joined(*packed)
    sides = call(side_kernel, [((SIDE, 128), BF16)] * 2, (), 1, 3)(place, east, west)
    sides = joined(*sides)
    sliced = call(slice_kernel, [((16, 128, 128), BF16)], [pltpu.VMEM((512, 128), F32)], 1, 2)(
        (2 * core + z).astype(jnp.int32).reshape(1), dictionary
    )
    sliced = lax.all_to_all(sliced, "lon", 0, 0, tiled=True)
    turned = call(turn_kernel, [((HALF, 512), BF16)], [pltpu.VMEM((4, 512, 128), F32)])(sliced)
    turned_other = flipped(turned, "lat", 2)
    x, edge = call(
        unpack_kernel,
        [((2 * PACK, MAIN), BF16), ((2 * PACK, 256), BF16)],
        [
            pltpu.VMEM((2 * PACK, MAIN), BF16),
            pltpu.VMEM((2 * PACK, 256), BF16),
            pltpu.VMEM((4, 4, PACK, 128), BF16),
            pltpu.VMEM((4, 4, SIDE, 128), BF16),
            pltpu.SemaphoreType.DMA((8,)),
        ],
        1,
        9,
        pltpu.HBM,
    )(place, *fields, *sides)

    work = [
        pltpu.VMEM((512, LANES), BF16),
        pltpu.VMEM((640, 256), BF16),
        pltpu.VMEM((512, LANES), F32),
    ]
    state = ((64, LANES), F32)
    limits = thresholds.reshape(1, 64)
    mine, moving, blocks, blocks_t = call(
        first_kernel, [state, state, ((640, 512), BF16), ((512, 640), BF16)], work, 1, 5
    )(place, turned, turned_other, x, edge)
    swap = [(i, i ^ 1) for i in range(4)]
    current = moving
    momentum_now = 1.0
    for _ in range(ITERS - 1):
        other = lax.ppermute(mine, "lat", swap)
        momentum_next = (1.0 + math.sqrt(1.0 + 4.0 * momentum_now * momentum_now)) / 2.0
        factor = (momentum_now - 1.0) / momentum_next
        momentum_now = momentum_next

        def step(*refs):
            middle_kernel(factor, *refs)

        mine, moving, current = call(step, [state, state, state], work, 1, 10)(
            place, mine, other, moving, current, limits, blocks_t, blocks, x, edge
        )
    other = lax.ppermute(mine, "lat", swap)
    positions = lax.axis_size("tm") * lax.axis_size("lat") * lon * 64

    def ending(*refs):
        last_kernel(1.0 / math.sqrt(positions), *refs)

    codes, grad = call(
        ending,
        [((64, 128), F32), ((16, 32, HALF), BF16)],
        [pltpu.VMEM((512, LANES), BF16), pltpu.VMEM((512, HALF), F32)],
        1,
        7,
    )(place, mine, other, moving, limits, blocks, x)
    grad = lax.all_to_all(grad, "lon", 0, 0, tiled=True)
    summed = call(add_kernel, [((32, HALF), F32)])(grad)
    others = [lax.ppermute(summed, "lat", [(i, i ^ flip) for i in range(4)]) for flip in (1, 2, 3)]
    gradient = call(
        place_kernel, [((4, 9984), F32)], [pltpu.VMEM((16, 32, 128), F32), pltpu.VMEM((64, 128), F32)], 1, 5
    )(place, summed, *others)
    return codes[:, :64].reshape(1, 64, 2, 32), gradient


def solution(mesh):
    placed = (P("tm", None, "lat", "lon"), P("lon", None), P("tm", None, "lat", "lon"), P())
    return jax.shard_map(
        program,
        mesh=mesh,
        in_specs=placed,
        out_specs=(P("tm", None, "lat", "lon"), P("lon", None)),
        check_vma=False,
    )
```

```python
import math

import jax
import jax.numpy as jnp
from jax import lax
from jax.experimental import pallas as pl
from jax.experimental.pallas import tpu as pltpu
from jax.sharding import PartitionSpec as P


ITERS = 2
STEP_SIZE = 0.5
F32 = jnp.float32
BF16 = jnp.bfloat16
COMBOS = [(h, a, b) for h in (0, 1) for a in (0, 1) for b in (0, 1)]
MAIN = 1024
LANES = 1280
HALF = 320
PACK = 384
SIDE = 96


def iota(shape, dim):
    return lax.broadcasted_iota(jnp.int32, shape, dim)


def dot(a, b):
    return jnp.dot(a, b, preferred_element_type=F32)


def dot_t(a, b):
    return lax.dot_general(a, b, (((1,), (1,)), ((), ())), preferred_element_type=F32)


def onehot(test):
    return jnp.where(test, 1.0, 0.0).astype(BF16)


def two(x):
    high = x.astype(BF16)
    return high, (x - high.astype(F32)).astype(BF16)


def three(x):
    high = x.astype(BF16)
    rest = x - high.astype(F32)
    middle = rest.astype(BF16)
    return high, middle, (rest - middle.astype(F32)).astype(BF16)


def call(kernel, outs, scratch=(), smem=0, n_in=1, space=pltpu.VMEM):
    vmem = pl.BlockSpec(memory_space=pltpu.VMEM)
    held = pl.BlockSpec(memory_space=space)
    specs = [pl.BlockSpec(memory_space=pltpu.SMEM)] * smem + [held] * (n_in - smem)
    shapes = [jax.ShapeDtypeStruct(s, d) for s, d in outs]
    return pl.pallas_call(
        kernel,
        out_shape=shapes if len(shapes) > 1 else shapes[0],
        in_specs=specs,
        out_specs=[vmem] * len(shapes) if len(shapes) > 1 else vmem,
        scratch_shapes=list(scratch),
        compiler_params=pltpu.CompilerParams(vmem_limit_bytes=16 * 1024 * 1024),
    )


def edge_kernel(x_ref, z_ref, west_ref, east_ref):
    high, low = two(z_ref[...])
    codes = jnp.concatenate([high, low], axis=0)
    row, col = iota((128, 128), 0), iota((128, 128), 1)
    for first, out_ref in ((0, west_ref), (28, east_ref)):
        total = jnp.zeros((80, 128), F32)
        wanted = (first + (col & 3)) * 4 + ((col >> 3) & 3)
        for r in range(8):
            pick = (row == wanted) & ((col >> 5) == r % 4) & (((col >> 2) & 1) == r // 4)
            total = total + dot(x_ref[r], onehot(pick))
        out_ref[0:80, :] = total.astype(BF16)
        lane = iota((64, 128), 1)
        pick = (lane < 8) & (iota((64, 128), 0) == (lane >> 2) * 32 + first + (lane & 3))
        narrow = dot(codes, onehot(pick))
        edge = narrow[0:8]
        for group in range(1, 16):
            edge = edge + pltpu.roll(narrow[group * 8 : group * 8 + 8], group * 8, 1)
        out_ref[80:96, :] = jnp.concatenate([edge, jnp.zeros((8, 128), F32)], axis=0).astype(BF16)


def pack_kernel(place_ref, x_ref, z_ref, own_ref, other_ref):
    row, col = iota((128, 128), 0), iota((128, 128), 1)
    order = onehot(((row & 3) * 32 + (row >> 2)) == col)
    lane = iota((80, 128), 1)
    high, low = two(z_ref[...])
    codes = jnp.concatenate([high, low], axis=1)
    for flip, out_ref in enumerate((own_ref, other_ref)):
        first = (place_ref[0] ^ flip) * 2
        split = [dot(x_ref[p2 * 4 + first + u_lo], order) for u_lo in range(2) for p2 in range(2)]
        for v in range(4):
            piece = jnp.zeros((80, 128), F32)
            for slot in range(4):
                by = ((slot - v) % 4) * 32
                moved = pltpu.roll(split[slot], by, 1) if by else split[slot]
                piece = jnp.where((lane >> 5) == slot, moved, piece)
            out_ref[v * 80 : v * 80 + 80, :] = piece.astype(BF16)
        out_ref[HALF:PACK, :] = codes


def side_kernel(place_ref, east_ref, west_ref, own_ref, other_ref):
    row, col = iota((128, 128), 0), iota((128, 128), 1)
    is_east = (col & 7) < 4
    within = ((col >> 3) & 1) * 4 + (col & 3)
    sides = []
    for part in range(2):
        pick = row == (2 * (col >> 4) + part) * 8 + within
        east = dot(east_ref[80:96, :], onehot(pick & is_east))
        west = dot(west_ref[80:96, :], onehot(pick & jnp.logical_not(is_east)))
        sides.append((east + west)[0:8])
    codes = jnp.concatenate(sides, axis=0).astype(BF16)
    for flip, out_ref in enumerate((own_ref, other_ref)):
        pick = row == ((place_ref[0] ^ flip) * 8 + (col >> 4)) * 8 + within
        east = dot(east_ref[0:80, :], onehot(pick & is_east))
        west = dot(west_ref[0:80, :], onehot(pick & jnp.logical_not(is_east)))
        out_ref[0:80, :] = (east + west).astype(BF16)
        out_ref[80:SIDE, :] = codes


def fetched(refs, held, arrived):
    copies = [pltpu.make_async_copy(ref, held.at[i], arrived.at[i]) for i, ref in enumerate(refs)]
    for copy in copies:
        copy.start()
    return copies


def unpack_kernel(place_ref, *refs):
    main_ref, token_ref, left_ref, hours, arrived = refs[4:]
    token_ref[...] = jnp.zeros((8, 128), F32)
    copies = fetched(refs[:4], hours, arrived)
    lane = iota((PACK, 128), 1)
    for pair in range(8):
        if pair % 2 == 0:
            copies[pair // 2].wait()
        even = hours[pair // 2, 2 * (pair % 2)].astype(F32)
        odd = hours[pair // 2, 2 * (pair % 2) + 1].astype(F32)
        lanes = slice(pair * 128, pair * 128 + 128)
        left_ref[0:PACK, lanes] = jnp.where(lane < 64, even, pltpu.roll(odd, 64, 1)).astype(BF16)
        left_ref[PACK : 2 * PACK, lanes] = jnp.where(lane < 64, pltpu.roll(even, 64, 1), odd).astype(BF16)
    lat, hour = 2 * place_ref[1] + place_ref[0], place_ref[2]
    for block in range(4):
        n = iota((1024, 256), 1) + block * 256
        slab = (((n >> 3) & 3) ^ hour) * 4 + (((n >> 1) & 3) ^ lat)
        source = slab * 64 + (n & 1) * 32 + (n >> 5)
        order = onehot(iota((1024, 256), 0) == source)
        main_ref[:, block * 256 : block * 256 + 256] = dot(left_ref[...], order).astype(BF16)


def unpack_side_kernel(place_ref, *refs):
    edge_ref, side_ref, edges, arrived = refs[5:]
    copies = fetched(refs[:4], edges, arrived)
    lat, hour = 2 * place_ref[1] + place_ref[0], place_ref[2]
    n = iota((256, 256), 1)
    slab = (((n >> 3) & 3) ^ hour) * 4 + (((n >> 1) & 3) ^ lat)
    order = onehot(iota((256, 256), 0) == slab * 16 + (n & 1) * 8 + (n >> 5))
    lane = iota((SIDE, 128), 1)
    for copy in copies:
        copy.wait()
    for half in range(2):
        slabs = [edges[half * 2 + s // 4, s % 4].astype(F32) for s in range(8)]
        for group in range(8):
            piece = jnp.zeros((SIDE, 128), F32)
            for s in range(8):
                by = ((s - group) % 8) * 16
                moved = pltpu.roll(slabs[s], by, 1) if by else slabs[s]
                piece = jnp.where((lane >> 4) == s, moved, piece)
            side_ref[group * 96 : group * 96 + 96, half * 128 : half * 128 + 128] = piece.astype(BF16)
    sides = dot(side_ref[...], order).astype(BF16)
    for group in range(8):
        at = (group // 4) * PACK + (group % 4) * 80
        edge_ref[at : at + 80, :] = sides[group * 96 : group * 96 + 80]
        at = (group // 4) * PACK + HALF + (group % 4) * 16
        edge_ref[at : at + 16, :] = sides[group * 96 + 80 : group * 96 + 96]


def dense(x):
    last = x[:, 256:384]
    lane = iota((16, 128), 1)
    last = jnp.where(lane < 64, last[0:16], pltpu.roll(last[16:32], 64, 1))
    return jnp.concatenate([x[:, 0:128], x[:, 128:256], last], axis=0)


def spread(x):
    last = x[64:80]
    last = jnp.concatenate([last, pltpu.roll(last, 64, 1)], axis=0)
    return jnp.concatenate([x[0:32], x[32:64], last], axis=1)


def slice_kernel(place_ref, d_ref, out_ref, rows_ref):
    rows_ref[...] = jnp.zeros((512, 128), F32)
    for i in range(78):
        h, half = i // 39, i % 39
        part = d_ref[:, i * 128 : i * 128 + 128].astype(F32)
        for k in range(4):
            at = (k * 2 + h) * 64 + half
            rows_ref[at : at + 1, :] = part[k : k + 1, :]
    which = iota((32, 128), 0)
    want = ((which >> 2) & 1) * 64 + ((which >> 1) & 1) * 32 + place_ref[0] * 8 + (which & 1) * 4 + (which >> 3)
    picked = dot_t(onehot(iota((32, 128), 1) == want), rows_ref[...].astype(BF16))
    lane = iota((4, 128), 1)
    for v in range(4):
        for k in range(4):
            pair = picked[v * 8 : v * 8 + 8, k * 128 : k * 128 + 128]
            turned = pltpu.roll(pair, 64, 1)
            even = jnp.where(lane < 64, pair[0:4], turned[4:8])
            odd = jnp.where(lane < 64, turned[0:4], pair[4:8])
            for ab in range(4):
                at = v * 32 + ab * 4 + k
                rows_ref[at : at + 1, :] = even[ab : ab + 1, :]
                rows_ref[at + 16 : at + 17, :] = odd[ab : ab + 1, :]
    row, col = iota((128, 384), 0), iota((128, 384), 1)
    total = jnp.zeros((32, 384), F32)
    for v in range(4):
        put = ((row & 63) < 40) & (col == v * 80 + (row >> 6) * 40 + (row & 63))
        total = total + dot(rows_ref[v * 32 : v * 32 + 32, :].astype(BF16), onehot(put))
    sent = dense(total).astype(BF16)
    for peer in range(16):
        out_ref[peer] = sent


def turn_kernel(in_ref, out_ref, rows_ref):
    for peer in range(16):
        part = spread(in_ref[peer].astype(F32))
        for hab in range(8):
            at = hab * 64 + peer * 4
            rows_ref[at : at + 4, :] = part[hab * 4 : hab * 4 + 4, :]
    out_ref[...] = rows_ref[...].T[0:HALF].astype(BF16)


def shifted_codes(codes, z_ref):
    lane = iota((1, LANES), 1)
    t, p = (lane >> 3) & 3, lane & 7
    for index, (h, a, b) in enumerate(COMBOS):
        by = 32 * b + 8 * h + a
        moved = pltpu.roll(codes, by, 1) if by else codes
        kept = jnp.where((t >= h) & (p >= a), moved, 0.0)
        z_ref[index * 64 : index * 64 + 64, :] = kept.astype(BF16)


def partial_adjoint(z, b_ref, bt_ref, x_ref, edge_ref, z_ref, r_ref, u_ref):
    for chunk in range(5):
        lanes = slice(chunk * 256, chunk * 256 + 256)
        codes = z_ref[:, lanes]
        for slot in range(2):
            rows = slice(slot * HALF, slot * HALF + HALF)
            held = pl.ds(pl.multiple_of((z ^ slot) * PACK, PACK), HALF)
            x = x_ref[held, lanes] if chunk < 4 else edge_ref[held, :]
            r_ref[rows, :] = (dot(b_ref[rows, :], codes) - x.astype(F32)).astype(BF16)
        u_ref[:, lanes] = dot(bt_ref[...], r_ref[...])
    lane = iota((1, LANES), 1)
    t, p = (lane >> 3) & 3, lane & 7
    total = u_ref[0:64, :]
    for index, (h, a, b) in enumerate(COMBOS[1:], 1):
        moved = pltpu.roll(u_ref[index * 64 : index * 64 + 64, :], LANES - (32 * b + 8 * h + a), 1)
        total = total + jnp.where((t < 4 - h) & (p < 8 - a), moved, 0.0)
    return total


def first_kernel(place_ref, own_ref, other_ref, x_ref, edge_ref, sum_ref, y_ref, b_ref, bt_ref, z_ref, r_ref, u_ref):
    b_ref[0:HALF, :] = own_ref[...]
    b_ref[HALF : 2 * HALF, :] = other_ref[...]
    bt_ref[...] = b_ref[...].T

    def rows_of(start, count):
        part = slice(start, start + count)
        return jnp.concatenate([x_ref[part, :], edge_ref[part, :]], axis=1).astype(F32)

    codes = rows_of(HALF, 64) + rows_of(PACK + HALF, 64)
    y_ref[...] = codes
    shifted_codes(codes, z_ref)
    sum_ref[...] = partial_adjoint(place_ref[1], b_ref, bt_ref, x_ref, edge_ref, z_ref, r_ref, u_ref)


def shrunk(moving, gradient, limits):
    same = iota((64, 64), 0) == iota((64, 64), 1)
    shrink = STEP_SIZE * jnp.sum(jnp.where(same, limits, 0.0), axis=1, keepdims=True)
    descent = moving - STEP_SIZE * gradient
    size = jnp.maximum(jnp.abs(descent) - shrink, 0.0)
    return jnp.where(descent < 0.0, -size, size)


def middle_kernel(factor, place_ref, mine_ref, other_ref, moving_ref, current_ref, limit_ref, bt_ref, b_ref, x_ref, edge_ref, sum_ref, y_ref, now_ref, z_ref, r_ref, u_ref):
    updated = shrunk(moving_ref[...], mine_ref[...] + other_ref[...], limit_ref[...])
    moving = updated + factor * (updated - current_ref[...])
    now_ref[...] = updated
    y_ref[...] = moving
    shifted_codes(moving, z_ref)
    sum_ref[...] = partial_adjoint(place_ref[1], b_ref, bt_ref, x_ref, edge_ref, z_ref, r_ref, u_ref)


def last_kernel(scale, place_ref, mine_ref, other_ref, moving_ref, limit_ref, b_ref, x_ref, codes_ref, grad_ref, z_ref, g_ref):
    codes = shrunk(moving_ref[...], mine_ref[...] + other_ref[...], limit_ref[...])
    core, z, t = place_ref[0], place_ref[1], place_ref[2]
    own = iota((MAIN, 128), 1)
    source = (own & 31) * 32 + t * 8 + (2 * z + core) * 2 + ((own >> 5) & 1)
    order = onehot((iota((MAIN, 128), 0) == source) & (own < 64))
    high, middle, low = three(codes[:, 0:MAIN])
    codes_ref[...] = (dot(high, order) + dot(middle, order)) + dot(low, order)
    shifted_codes(codes, z_ref)
    z_main = z_ref[:, 0:MAIN]
    x = x_ref[pl.ds(pl.multiple_of(z * PACK, 16), HALF), :]
    residual = (dot(b_ref[0:HALF, :], z_main) - x.astype(F32)).astype(BF16)
    filled = jnp.concatenate([residual, jnp.zeros((64, MAIN), BF16)], axis=0)
    g_ref[...] = dot_t(z_main, filled) * scale
    for peer in range(16):
        parts = [g_ref[hab * 64 + peer * 4 : hab * 64 + peer * 4 + 4, :] for hab in range(8)]
        grad_ref[peer] = dense(jnp.concatenate(parts, axis=0)).astype(BF16)


def add_kernel(in_ref, out_ref):
    total = in_ref[0].astype(F32)
    for peer in range(1, 16):
        total = total + in_ref[peer].astype(F32)
    out_ref[...] = total


def place_kernel(place_ref, own_ref, core_ref, z_ref, both_ref, out_ref, parts_ref, rows_ref):
    core, z = place_ref[0], place_ref[1]
    for flip, piece in enumerate((own_ref, core_ref, z_ref, both_ref)):
        u = 2 * (core ^ (flip & 1)) + (z ^ (flip >> 1))
        whole = spread(piece[...])
        for v in range(4):
            moved = pltpu.roll(whole, 384 - v * 80, 1) if v else whole
            parts_ref[u * 4 + v] = moved[:, 0:128]
    for k in range(4):
        for h in range(2):
            for ab in range(4):
                row = (h * 4 + ab) * 4 + k
                for uv in range(16):
                    at = (ab // 2) * 32 + (uv // 4) * 8 + (ab % 2) * 4 + uv % 4
                    rows_ref[at : at + 1, :] = parts_ref[uv, row : row + 1, :]
            even = rows_ref[...]
            odd = pltpu.roll(even, 88, 1)
            turned = jnp.concatenate([even, odd], axis=0).T
            for i in range(39):
                lanes = slice((h * 39 + i) * 128, (h * 39 + i) * 128 + 128)
                out_ref[k : k + 1, lanes] = turned[i : i + 1, :]


def program(signal, dictionary, codes_init, thresholds):
    lat, tm = lax.axis_index("lat"), lax.axis_index("tm")
    z, core = lat // 2, lat % 2
    place = jnp.stack([core, z, tm]).astype(jnp.int32)
    lon = lax.axis_size("lon")

    ring = [[(i, (i + by) % lon) for i in range(lon)] for by in (-1, 1)]

    def flipped(block, axis, by):
        return lax.ppermute(block, axis, [(i, i ^ by) for i in range(4)])

    rows = signal[0].reshape(39, 2, 8, 128).transpose(2, 1, 0, 3)
    rows = jnp.pad(rows, ((0, 0), (0, 0), (0, 1), (0, 0))).reshape(8, 80, 128)
    start = codes_init[0].reshape(64, 64)

    def joined(kept, given):
        beside = flipped(given, "lat", 1)
        bands = [kept, beside, flipped(kept, "lat", 2), flipped(beside, "lat", 2)]
        hour = jnp.stack(bands)
        return [hour] + [flipped(hour, "tm", by) for by in (1, 2, 3)]

    west, east = call(edge_kernel, [((SIDE, 128), BF16)] * 2, n_in=2)(rows, start)
    east, west = lax.ppermute(west, "lon", ring[0]), lax.ppermute(east, "lon", ring[1])
    packed = call(pack_kernel, [((PACK, 128), BF16)] * 2, (), 1, 3)(place, rows, start)
    fields = joined(*packed)
    sides = call(side_kernel, [((SIDE, 128), BF16)] * 2, (), 1, 3)(place, east, west)
    sides = joined(*sides)
    sliced = call(slice_kernel, [((16, 80, 128), BF16)], [pltpu.VMEM((512, 128), F32)], 1, 2)(
        (2 * core + z).astype(jnp.int32).reshape(1), dictionary
    )
    sliced = lax.all_to_all(sliced, "lon", 0, 0, tiled=True)
    turned = call(turn_kernel, [((HALF, 512), BF16)], [pltpu.VMEM((512, 384), F32)])(sliced)
    turned_other = flipped(turned, "lat", 2)
    x, token = call(
        unpack_kernel,
        [((2 * PACK, MAIN), BF16), ((8, 128), F32)],
        [
            pltpu.VMEM((2 * PACK, MAIN), BF16),
            pltpu.VMEM((4, 4, PACK, 128), BF16),
            pltpu.SemaphoreType.DMA((4,)),
        ],
        1,
        5,
        pltpu.HBM,
    )(place, *fields)
    edge = call(
        unpack_side_kernel,
        [((2 * PACK, 256), BF16)],
        [
            pltpu.VMEM((2 * PACK, 256), BF16),
            pltpu.VMEM((4, 4, SIDE, 128), BF16),
            pltpu.SemaphoreType.DMA((4,)),
        ],
        1,
        6,
        pltpu.HBM,
    )(place, *sides, token)

    work = [
        pltpu.VMEM((512, LANES), BF16),
        pltpu.VMEM((640, 256), BF16),
        pltpu.VMEM((512, LANES), F32),
    ]
    state = ((64, LANES), F32)
    limits = thresholds.reshape(1, 64)
    mine, moving, blocks, blocks_t = call(
        first_kernel, [state, state, ((640, 512), BF16), ((512, 640), BF16)], work, 1, 5
    )(place, turned, turned_other, x, edge)
    swap = [(i, i ^ 1) for i in range(4)]
    current = moving
    momentum_now = 1.0
    for _ in range(ITERS - 1):
        other = lax.ppermute(mine, "lat", swap)
        momentum_next = (1.0 + math.sqrt(1.0 + 4.0 * momentum_now * momentum_now)) / 2.0
        factor = (momentum_now - 1.0) / momentum_next
        momentum_now = momentum_next

        def step(*refs):
            middle_kernel(factor, *refs)

        mine, moving, current = call(step, [state, state, state], work, 1, 10)(
            place, mine, other, moving, current, limits, blocks_t, blocks, x, edge
        )
    other = lax.ppermute(mine, "lat", swap)
    positions = lax.axis_size("tm") * lax.axis_size("lat") * lon * 64

    def ending(*refs):
        last_kernel(1.0 / math.sqrt(positions), *refs)

    codes, grad = call(
        ending,
        [((64, 128), F32), ((16, 80, 128), BF16)],
        [pltpu.VMEM((512, LANES), BF16), pltpu.VMEM((512, 384), F32)],
        1,
        7,
    )(place, mine, other, moving, limits, blocks, x)
    grad = lax.all_to_all(grad, "lon", 0, 0, tiled=True)
    summed = call(add_kernel, [((80, 128), F32)])(grad)
    others = [lax.ppermute(summed, "lat", [(i, i ^ flip) for i in range(4)]) for flip in (1, 2, 3)]
    gradient = call(
        place_kernel, [((4, 9984), F32)], [pltpu.VMEM((16, 32, 128), F32), pltpu.VMEM((64, 128), F32)], 1, 5
    )(place, summed, *others)
    return codes[:, :64].reshape(1, 64, 2, 32), gradient


def solution(mesh):
    placed = (P("tm", None, "lat", "lon"), P("lon", None), P("tm", None, "lat", "lon"), P())
    return jax.shard_map(
        program,
        mesh=mesh,
        in_specs=placed,
        out_specs=(P("tm", None, "lat", "lon"), P("lon", None)),
        check_vma=False,
    )
```
